1024 devices in a mesh: vec: 64 (over y, x_lo, core), field: 16 (over z, x_hi).
Axes of the slice: x: 8 (x_hi: 2, x_lo: 4; x = x_hi * 4 + x_lo), y: 8, z: 8, core: 2. Of those that a mesh axis runs over, the one named last changes fastest.
Arguments:
- vectors: float32 [4096, 24576], P('vec', 'field'), may hold values from -6 to 6
Outputs:
- first_tensor: float32 [4096, 4096], P(('vec', 'field'))
- second_tensor: float32 [4096, 4096], P(('vec', 'field'))
The draws below stay inside these ranges and needn't reach their ends.
All inputs are finite; a program needn't handle non-finite values.
Results may differ from the reference program's by a relative error of at most 0.000098.
Values sent between devices are 32-bit elements; how exact they have to be, the bound alone decides.
No kernel may reach another device: no remote copies, remote signals or barrier semaphores. Data moves between devices by JAX's collectives and lax.ppermute only.
A program may use at most 64 MiB of HBM per device.

```python
import jax
import jax.numpy as jnp
from jax import lax

NV = 64
VECS = 4096
FIELDS = 24576
N_VEC = 64


def levels(own_key, extent, split, low, top_value):
    factor_of, own = 1.0, jax.random.fold_in(own_key, 6)
    for dim, blocks in split:
        steps = jnp.exp(jax.random.uniform(jax.random.fold_in(own, dim), (blocks,), jnp.float32, low / len(split), top_value / len(split)))
        factor_of = factor_of * jnp.repeat(steps, extent[dim] // blocks).reshape([-1 if axis == dim else 1 for axis in range(len(extent))])
    return factor_of


def normal_values(rng, extent, deviation, bound, pieces=(), dtype=jnp.bfloat16):
    loudness = levels(rng, extent, pieces, -0.22, 0.18) if pieces else 1.0
    values = jax.random.normal(rng, extent, jnp.float32) * deviation * loudness
    return jnp.minimum(jnp.maximum(values, -bound), bound).astype(dtype)


def setup_inputs(seed: int = 0) -> dict:
    seeds = jax.random.split(jax.random.key(seed), 2)
    vectors = normal_values(seeds[0], (VECS, FIELDS), 1.0, 6.0, ((0, 64), (1, 16)), jnp.float32)
    return {"vectors": vectors}


def triple_block(first, partner, third):
    product = (first[:, None, :] * partner[None, :, :]).reshape(first.shape[0] * partner.shape[0], first.shape[1])
    result = lax.dot_general(product, third, (((1,), (1,)), ((), ())), precision=lax.Precision.HIGHEST, preferred_element_type=jnp.float32)
    return result.reshape(first.shape[0], partner.shape[0] * third.shape[0])

def reference(vectors):
    blocks = vectors.reshape(N_VEC, NV, vectors.shape[1])
    following = jnp.roll(blocks, -1, axis=0)
    further = jnp.roll(blocks, -2, axis=0)
    previous = jnp.roll(blocks, 1, axis=0)
    scale = 1.0 / jnp.sqrt(jnp.float32(vectors.shape[1]))
    first_tensor = lax.map(lambda items: triple_block(items[0], items[1], items[2]), (blocks, following, further))
    second_tensor = lax.map(lambda items: triple_block(items[0], items[1], items[2]), (blocks, previous, following))
    first_tensor = first_tensor.reshape(N_VEC * NV, NV * NV) * scale
    second_tensor = second_tensor.reshape(N_VEC * NV, NV * NV) * scale
    return (first_tensor, second_tensor)
```

```python
import math

import jax
import jax.numpy as jnp
from jax import lax
from jax.experimental import pallas as pl
from jax.experimental.pallas import tpu as pltpu
from jax.sharding import PartitionSpec as P

GROUP = 16


def passed_along(x, axis, by):
    peers = lax.axis_size(axis)
    return lax.ppermute(x, axis, [(i, (i + by) % peers) for i in range(peers)])


def two_halves(x):
    high = x.astype(jnp.bfloat16)
    return high, (x - high.astype(jnp.float32)).astype(jnp.bfloat16)


def triple_kernel(scale, a_ref, b_ref, c_ref, out_ref, w_ref):
    rows = b_ref.shape[0]
    w_ref[...] = jnp.concatenate(two_halves(c_ref[...]), 0).T
    first_half = lax.broadcasted_iota(jnp.int32, (rows, 2 * rows), 1) < rows

    def step(g, carry):
        highs, lows = [], []
        for u in range(GROUP):
            high, low = two_halves(a_ref[pl.ds(g * GROUP + u, 1), :] * b_ref[...])
            highs.append(high)
            lows.append(low)
        w = w_ref[...]
        r = jnp.dot(jnp.concatenate(highs, 0), w, preferred_element_type=jnp.float32)
        r = r + jnp.dot(jnp.concatenate(lows, 0), w, preferred_element_type=jnp.float32)
        r = (r + pltpu.roll(r, rows, 1)) * scale
        for u in range(GROUP // 2):
            even = r[2 * u * rows : (2 * u + 1) * rows]
            odd = r[(2 * u + 1) * rows : (2 * u + 2) * rows]
            out_ref[g * (GROUP // 2) + u] = jnp.where(first_half, even, odd)
        return carry

    lax.fori_loop(0, rows // GROUP, step, 0)


def triples(a, b, c, scale):
    rows, fields = b.shape
    return pl.pallas_call(
        lambda *refs: triple_kernel(scale, *refs),
        name="triples",
        out_shape=jax.ShapeDtypeStruct((rows // 2, rows, 2 * rows), jnp.float32),
        in_specs=[pl.BlockSpec(memory_space=pltpu.VMEM)] * 3,
        out_specs=pl.BlockSpec(memory_space=pltpu.VMEM),
        scratch_shapes=[pltpu.VMEM((fields, 2 * rows), jnp.bfloat16)],
        compiler_params=pltpu.CompilerParams(vmem_limit_bytes=40 * 2**20),
        cost_estimate=pl.CostEstimate(
            flops=8 * rows**3 * fields, bytes_accessed=4 * (rows**3 + 3 * rows * fields), transcendentals=0
        ),
    )(a, b, c)


def per_device(vectors):
    parts = lax.axis_size("field")
    rows = vectors.shape[0]
    pairs = rows // parts // 2
    scale = 1.0 / math.sqrt(vectors.shape[1] * parts)
    previous = passed_along(vectors, "vec", 1)
    following = passed_along(vectors, "vec", -1)
    partial = triples(previous, vectors, following, scale)
    pieces = partial.reshape(parts, pairs, rows, 2 * rows)
    arrived = lax.all_to_all(pieces, "field", split_axis=0, concat_axis=0, tiled=True)
    mine = arrived.sum(axis=0)
    first = passed_along(mine, "vec", -1)
    first = first.reshape(pairs, rows, 2, rows).transpose(0, 2, 1, 3).reshape(2 * pairs, rows * rows)
    split = mine.reshape(pairs, parts, rows // parts, 2 * rows).transpose(1, 0, 2, 3)
    turned = lax.all_to_all(split, "field", split_axis=0, concat_axis=0, tiled=True)
    turned = turned.reshape(rows // 2, rows // parts, 2 * rows)
    second = jnp.transpose(turned, (1, 0, 2)).reshape(rows // parts, rows * rows)
    return (first, second)


def solution(mesh):
    placed = (P("vec", "field"),)
    return jax.shard_map(
        per_device,
        mesh=mesh,
        in_specs=placed,
        out_specs=(P(("vec", "field"), None), P(("vec", "field"), None)),
        check_vma=False,
    )
```

```python
import math

import jax
import jax.numpy as jnp
from jax import lax
from jax.experimental import pallas as pl
from jax.experimental.pallas import tpu as pltpu
from jax.sharding import PartitionSpec as P

GROUP = 16


def passed_along(x, axis, by):
    peers = lax.axis_size(axis)
    return lax.ppermute(x, axis, [(i, (i + by) % peers) for i in range(peers)])


def two_halves(x):
    high = x.astype(jnp.bfloat16)
    return high, (x - high.astype(jnp.float32)).astype(jnp.bfloat16)


def triple_kernel(scale, a_ref, b_hbm, c_ref, out_ref, b_ref, w_ref, arrived):
    rows = b_ref.shape[0]
    fetch = pltpu.make_async_copy(b_hbm, b_ref, arrived)
    fetch.start()
    w_ref[...] = jnp.concatenate(two_halves(c_ref[...]), 0).T
    first_half = lax.broadcasted_iota(jnp.int32, (rows, 2 * rows), 1) < rows
    fetch.wait()

    def step(g, carry):
        highs, lows = [], []
        for u in range(GROUP):
            high, low = two_halves(a_ref[pl.ds(g * GROUP + u, 1), :] * b_ref[...])
            highs.append(high)
            lows.append(low)
        w = w_ref[...]
        r = jnp.dot(jnp.concatenate(highs, 0), w, preferred_element_type=jnp.float32)
        r = r + jnp.dot(jnp.concatenate(lows, 0), w, preferred_element_type=jnp.float32)
        r = (r + pltpu.roll(r, rows, 1)) * scale
        for u in range(GROUP // 2):
            even = r[2 * u * rows : (2 * u + 1) * rows]
            odd = r[(2 * u + 1) * rows : (2 * u + 2) * rows]
            out_ref[g * (GROUP // 2) + u] = jnp.where(first_half, even, odd)
        return carry

    lax.fori_loop(0, rows // GROUP, step, 0)


def in_vmem(count):
    return [pl.BlockSpec(memory_space=pltpu.VMEM)] * count


def triples(a, b, c, scale):
    rows, fields = b.shape
    return pl.pallas_call(
        lambda *refs: triple_kernel(scale, *refs),
        name="triples",
        out_shape=jax.ShapeDtypeStruct((rows // 2, rows, 2 * rows), jnp.float32),
        in_specs=in_vmem(1) + [pl.BlockSpec(memory_space=pltpu.HBM)] + in_vmem(1),
        out_specs=pl.BlockSpec(memory_space=pltpu.VMEM),
        scratch_shapes=[
            pltpu.VMEM((rows, fields), jnp.float32),
            pltpu.VMEM((fields, 2 * rows), jnp.bfloat16),
            pltpu.SemaphoreType.DMA,
        ],
        compiler_params=pltpu.CompilerParams(vmem_limit_bytes=40 * 2**20),
        cost_estimate=pl.CostEstimate(
            flops=8 * rows**3 * fields, bytes_accessed=4 * (rows**3 + 3 * rows * fields), transcendentals=0
        ),
    )(a, b, c)


def regroup_kernel(half_ref, arrived_ref, send_ref, own_ref, other_ref, sum_ref):
    pairs, rows, lanes = sum_ref.shape
    per_owner = rows // send_ref.shape[0]
    sum_ref[...] = jnp.sum(arrived_ref[...], axis=0)
    for g in range(send_ref.shape[0]):
        for p in range(pairs):
            send_ref[g, p * per_owner : (p + 1) * per_owner] = sum_ref[p, g * per_owner : (g + 1) * per_owner]
    half = half_ref[0]
    for p in range(pairs // 2):
        own_ref[p] = sum_ref[half * (pairs // 2) + p]
        other_ref[p] = sum_ref[(1 - half) * (pairs // 2) + p]


def regroup(half, arrived, parts):
    _, pairs, rows, lanes = arrived.shape
    kept = jax.ShapeDtypeStruct((pairs // 2, rows, lanes), jnp.float32)
    return pl.pallas_call(
        regroup_kernel,
        name="regroup",
        out_shape=(jax.ShapeDtypeStruct((parts, pairs * rows // parts, lanes), jnp.float32), kept, kept),
        in_specs=[pl.BlockSpec(memory_space=pltpu.SMEM)] + in_vmem(1),
        out_specs=tuple(in_vmem(3)),
        scratch_shapes=[pltpu.VMEM((pairs, rows, lanes), jnp.float32)],
        compiler_params=pltpu.CompilerParams(vmem_limit_bytes=8 * 2**20),
    )(half, arrived)


def first_kernel(own_ref, other_ref, out_ref, sum_ref, row_ref):
    pairs, rows, lanes = own_ref.shape
    left = lax.broadcasted_iota(jnp.int32, (rows // 2, lanes), 1) < lanes // 2
    for p in range(pairs):
        sum_ref[p * rows : (p + 1) * rows] = own_ref[p] + other_ref[p]
    for p in range(pairs):
        even = sum_ref[pl.ds(p * rows, rows // 2, stride=2), :]
        odd = sum_ref[pl.ds(p * rows + 1, rows // 2, stride=2), :]
        row_ref[p * rows : p * rows + rows // 2] = jnp.where(left, even, pltpu.roll(odd, lanes // 2, 1))
        row_ref[p * rows + rows // 2 : (p + 1) * rows] = jnp.where(left, pltpu.roll(even, lanes // 2, 1), odd)
    for c in range(rows // 2):
        out_ref[:, c * lanes : (c + 1) * lanes] = row_ref[pl.ds(c, 2 * pairs, stride=rows // 2), :]


def first_rows(own, other):
    pairs, rows, lanes = own.shape
    return pl.pallas_call(
        first_kernel,
        name="first_rows",
        out_shape=jax.ShapeDtypeStruct((2 * pairs, rows * lanes // 2), jnp.float32),
        in_specs=in_vmem(2),
        out_specs=pl.BlockSpec(memory_space=pltpu.VMEM),
        scratch_shapes=[pltpu.VMEM((pairs * rows, lanes), jnp.float32)] * 2,
        compiler_params=pltpu.CompilerParams(vmem_limit_bytes=4 * 2**20),
    )(own, other)


def second_kernel(turned_ref, out_ref):
    parts, height, lanes = turned_ref.shape
    per_owner = out_ref.shape[0]
    pairs = height // per_owner
    for z in range(parts // 2):
        for p in range(pairs):
            c = z * pairs + p
            rows = slice(p * per_owner, (p + 1) * per_owner)
            out_ref[:, c * lanes : (c + 1) * lanes] = turned_ref[2 * z, rows] + turned_ref[2 * z + 1, rows]


def second_rows(turned, per_owner):
    parts, height, lanes = turned.shape
    return pl.pallas_call(
        second_kernel,
        name="second_rows",
        out_shape=jax.ShapeDtypeStruct((per_owner, parts // 2 * height // per_owner * lanes), jnp.float32),
        in_specs=in_vmem(1),
        out_specs=pl.BlockSpec(memory_space=pltpu.VMEM),
        compiler_params=pltpu.CompilerParams(vmem_limit_bytes=4 * 2**20),
    )(turned)


def per_device(vectors):
    blocks, parts = lax.axis_size("vec"), lax.axis_size("field")
    rows = vectors.shape[0]
    scale = 1.0 / math.sqrt(vectors.shape[1] * parts)
    previous = passed_along(vectors, "vec", 1)
    following = passed_along(vectors, "vec", -1)
    partial = triples(previous, vectors, following, scale)
    along_z = [[2 * z + half for z in range(parts // 2)] for half in range(2)]
    pieces = partial.reshape(parts // 2, rows // parts, rows, 2 * rows)
    arrived = lax.all_to_all(pieces, "field", 0, 0, axis_index_groups=along_z, tiled=True)
    half = lax.rem(lax.axis_index("field"), 2).reshape(1)
    send, own, other = regroup(half, arrived, parts)
    turned = lax.all_to_all(send, "field", split_axis=0, concat_axis=0, tiled=True)
    crossed = [
        (b * parts + f, (b - 1) % blocks * parts + (f ^ 1)) for b in range(blocks) for f in range(parts)
    ]
    own = passed_along(own, "vec", -1)
    other = lax.ppermute(other, ("vec", "field"), crossed)
    return (first_rows(own, other), second_rows(turned, rows // parts))


def solution(mesh):
    placed = (P("vec", "field"),)
    return jax.shard_map(
        per_device,
        mesh=mesh,
        in_specs=placed,
        out_specs=(P(("vec", "field"), None), P(("vec", "field"), None)),
        check_vma=False,
    )
```

```python
import math

import jax
import jax.numpy as jnp
from jax import lax
from jax.experimental import pallas as pl
from jax.experimental.pallas import tpu as pltpu
from jax.sharding import PartitionSpec as P


STEPS = 4


def passed_along(x, axis, by):
    peers = lax.axis_size(axis)
    return lax.ppermute(x, axis, [(i, (i + by) % peers) for i in range(peers)])


def two_halves(x):
    high = x.astype(jnp.bfloat16)
    return high, (x - high.astype(jnp.float32)).astype(jnp.bfloat16)


def in_vmem(count):
    return [pl.BlockSpec(memory_space=pltpu.VMEM)] * count


def fetch_kernel(in_ref, out_ref):
    out_ref[...] = in_ref[...]


def fetched(x):
    return pl.pallas_call(
        fetch_kernel,
        name="fetch",
        out_shape=jax.ShapeDtypeStruct(x.shape, x.dtype),
        in_specs=in_vmem(1),
        out_specs=pl.BlockSpec(memory_space=pltpu.VMEM),
        compiler_params=pltpu.CompilerParams(vmem_limit_bytes=4 * 2**20),
        cost_estimate=pl.CostEstimate(flops=0, bytes_accessed=2 * x.size * 4, transcendentals=0),
    )(x)


def triple_kernel(scale, a_ref, b_ref, c_ref, out_ref, w_ref):
    rows = b_ref.shape[0]
    group = 2 * out_ref.shape[0]

    @pl.when(pl.program_id(0) == 0)
    def _():
        w_ref[...] = jnp.concatenate(two_halves(c_ref[...]), 0).T

    first_half = lax.broadcasted_iota(jnp.int32, (rows, 2 * rows), 1) < rows
    highs, lows = [], []
    for u in range(group):
        high, low = two_halves(a_ref[pl.ds(pl.program_id(0) * group + u, 1), :] * b_ref[...])
        highs.append(high)
        lows.append(low)
    w = w_ref[...]
    r = jnp.dot(jnp.concatenate(highs, 0), w, preferred_element_type=jnp.float32)
    r = r + jnp.dot(jnp.concatenate(lows, 0), w, preferred_element_type=jnp.float32)
    r = (r + pltpu.roll(r, rows, 1)) * scale
    for u in range(group // 2):
        even = r[2 * u * rows : (2 * u + 1) * rows]
        odd = r[(2 * u + 1) * rows : (2 * u + 2) * rows]
        out_ref[u] = jnp.where(first_half, even, odd)


def triples(a, b, c, scale):
    rows, fields = b.shape
    return pl.pallas_call(
        lambda *refs: triple_kernel(scale, *refs),
        name="triples",
        grid=(STEPS,),
        out_shape=jax.ShapeDtypeStruct((rows // 2, rows, 2 * rows), jnp.float32),
        in_specs=in_vmem(3),
        out_specs=pl.BlockSpec((rows // 2 // STEPS, rows, 2 * rows), lambda s: (s, 0, 0)),
        scratch_shapes=[pltpu.VMEM((fields, 2 * rows), jnp.bfloat16)],
        compiler_params=pltpu.CompilerParams(vmem_limit_bytes=40 * 2**20),
        cost_estimate=pl.CostEstimate(
            flops=8 * rows**3 * fields, bytes_accessed=4 * (rows**3 + 3 * rows * fields), transcendentals=0
        ),
    )(a, b, c)


def regroup_kernel(half_ref, arrived_ref, send_ref, own_ref, other_ref, sum_ref):
    pairs, rows, _ = sum_ref.shape
    per_owner = rows // send_ref.shape[0]
    sum_ref[...] = jnp.sum(arrived_ref[...], axis=0)
    for g in range(send_ref.shape[0]):
        for p in range(pairs):
            send_ref[g, p * per_owner : (p + 1) * per_owner] = sum_ref[p, g * per_owner : (g + 1) * per_owner]
    half = half_ref[0]
    for p in range(pairs // 2):
        own_ref[p] = sum_ref[half * (pairs // 2) + p]
        other_ref[p] = sum_ref[(1 - half) * (pairs // 2) + p]


def regroup(half, arrived, parts):
    _, pairs, rows, lanes = arrived.shape
    kept = jax.ShapeDtypeStruct((pairs // 2, rows, lanes), jnp.float32)
    return pl.pallas_call(
        regroup_kernel,
        name="regroup",
        out_shape=(jax.ShapeDtypeStruct((parts, pairs * rows // parts, lanes), jnp.float32), kept, kept),
        in_specs=[pl.BlockSpec(memory_space=pltpu.SMEM)] + in_vmem(1),
        out_specs=tuple(in_vmem(3)),
        scratch_shapes=[pltpu.VMEM((pairs, rows, lanes), jnp.float32)],
        compiler_params=pltpu.CompilerParams(vmem_limit_bytes=8 * 2**20),
    )(half, arrived)


def finish_kernel(own_ref, other_ref, turned_ref, first_ref, second_ref, sum_ref, row_ref):
    pairs, rows, lanes = own_ref.shape
    left = lax.broadcasted_iota(jnp.int32, (rows // 2, lanes), 1) < lanes // 2
    for p in range(pairs):
        sum_ref[p * rows : (p + 1) * rows] = own_ref[p] + other_ref[p]
    for p in range(pairs):
        even = sum_ref[pl.ds(p * rows, rows // 2, stride=2), :]
        odd = sum_ref[pl.ds(p * rows + 1, rows // 2, stride=2), :]
        row_ref[p * rows : p * rows + rows // 2] = jnp.where(left, even, pltpu.roll(odd, lanes // 2, 1))
        row_ref[p * rows + rows // 2 : (p + 1) * rows] = jnp.where(left, pltpu.roll(even, lanes // 2, 1), odd)
    for c in range(rows // 2):
        first_ref[:, c * lanes : (c + 1) * lanes] = row_ref[pl.ds(c, 2 * pairs, stride=rows // 2), :]

    parts, height, _ = turned_ref.shape
    per_owner = second_ref.shape[0]
    pairs = height // per_owner
    for z in range(parts // 2):
        for p in range(pairs):
            c = z * pairs + p
            at = slice(p * per_owner, (p + 1) * per_owner)
            second_ref[:, c * lanes : (c + 1) * lanes] = turned_ref[2 * z, at] + turned_ref[2 * z + 1, at]


def finish(own, other, turned):
    pairs, rows, lanes = own.shape
    out = jax.ShapeDtypeStruct((2 * pairs, rows * lanes // 2), jnp.float32)
    return pl.pallas_call(
        finish_kernel,
        name="finish",
        out_shape=(out, out),
        in_specs=in_vmem(3),
        out_specs=tuple(in_vmem(2)),
        scratch_shapes=[pltpu.VMEM((pairs * rows, lanes), jnp.float32)] * 2,
        compiler_params=pltpu.CompilerParams(vmem_limit_bytes=4 * 2**20),
    )(own, other, turned)


def per_device(vectors):
    blocks, parts = lax.axis_size("vec"), lax.axis_size("field")
    rows = vectors.shape[0]
    scale = 1.0 / math.sqrt(vectors.shape[1] * parts)
    previous = passed_along(vectors, "vec", 1)
    following = passed_along(vectors, "vec", -1)
    partial = triples(previous, fetched(vectors), following, scale)
    along_z = [[2 * z + half for z in range(parts // 2)] for half in range(2)]
    pieces = partial.reshape(parts // 2, rows // parts, rows, 2 * rows)
    arrived = lax.all_to_all(pieces, "field", 0, 0, axis_index_groups=along_z, tiled=True)
    half = (lax.axis_index("field") & 1).reshape(1)
    send, own, other = regroup(half, arrived, parts)
    crossed = [(b * parts + f, (b - 1) % blocks * parts + (f ^ 1)) for b in range(blocks) for f in range(parts)]
    turned = lax.all_to_all(send, "field", split_axis=0, concat_axis=0, tiled=True)
    other = lax.ppermute(other, ("vec", "field"), crossed)
    own = passed_along(own, "vec", -1)
    return finish(own, other, turned)


def solution(mesh):
    placed = (P("vec", "field"),)
    return jax.shard_map(
        per_device,
        mesh=mesh,
        in_specs=placed,
        out_specs=(P(("vec", "field"), None), P(("vec", "field"), None)),
        check_vma=False,
    )
```

```python
import math

import jax
import jax.numpy as jnp
from jax import lax
from jax.experimental import pallas as pl
from jax.experimental.pallas import tpu as pltpu
from jax.sharding import PartitionSpec as P


GROUP = 16


def passed_along(x, axis, by):
    peers = lax.axis_size(axis)
    return lax.ppermute(x, axis, [(i, (i + by) % peers) for i in range(peers)])


def two_halves(x):
    high = x.astype(jnp.bfloat16)
    return high, (x - high.astype(jnp.float32)).astype(jnp.bfloat16)


def in_vmem(count):
    return [pl.BlockSpec(memory_space=pltpu.VMEM)] * count


def fetch_kernel(in_ref, out_ref):
    out_ref[...] = in_ref[...]


def fetched(x):
    return pl.pallas_call(
        fetch_kernel,
        name="fetch",
        out_shape=jax.ShapeDtypeStruct(x.shape, x.dtype),
        in_specs=in_vmem(1),
        out_specs=pl.BlockSpec(memory_space=pltpu.VMEM),
        compiler_params=pltpu.CompilerParams(vmem_limit_bytes=4 * 2**20),
        cost_estimate=pl.CostEstimate(flops=0, bytes_accessed=2 * x.size * 4, transcendentals=0),
    )(x)


def weights_kernel(c_ref, w_ref):
    w_ref[...] = jnp.concatenate(two_halves(c_ref[...]), 0).T


def weights(c):
    rows, fields = c.shape
    return pl.pallas_call(
        weights_kernel,
        name="weights",
        out_shape=jax.ShapeDtypeStruct((fields, 2 * rows), jnp.bfloat16),
        in_specs=in_vmem(1),
        out_specs=pl.BlockSpec(memory_space=pltpu.VMEM),
        compiler_params=pltpu.CompilerParams(vmem_limit_bytes=8 * 2**20),
        cost_estimate=pl.CostEstimate(flops=c.size, bytes_accessed=8 * c.size, transcendentals=0),
    )(c)


def triple_kernel(scale, run, stride, start_ref, a_ref, b_ref, w_ref, out_ref):
    rows = b_ref.shape[0]
    first_half = lax.broadcasted_iota(jnp.int32, (rows, 2 * rows), 1) < rows
    start = start_ref[0] + pl.program_id(0) * (GROUP // run * stride)
    highs, lows = [], []
    for u in range(GROUP):
        high, low = two_halves(a_ref[pl.ds(start + u // run * stride + u % run, 1), :] * b_ref[...])
        highs.append(high)
        lows.append(low)
    w = w_ref[...]
    r = jnp.dot(jnp.concatenate(highs, 0), w, preferred_element_type=jnp.float32)
    r = r + jnp.dot(jnp.concatenate(lows, 0), w, preferred_element_type=jnp.float32)
    r = (r + pltpu.roll(r, rows, 1)) * scale
    for u in range(GROUP // 2):
        even = r[2 * u * rows : (2 * u + 1) * rows]
        odd = r[(2 * u + 1) * rows : (2 * u + 2) * rows]
        out_ref[u] = jnp.where(first_half, even, odd)


def triples(start, a, b, w, scale, steps, run, stride):
    rows, fields = b.shape
    return pl.pallas_call(
        lambda *refs: triple_kernel(scale, run, stride, *refs),
        name="triples",
        grid=(steps,),
        out_shape=jax.ShapeDtypeStruct((steps * GROUP // 2, rows, 2 * rows), jnp.float32),
        in_specs=[pl.BlockSpec(memory_space=pltpu.SMEM)] + in_vmem(3),
        out_specs=pl.BlockSpec((GROUP // 2, rows, 2 * rows), lambda s: (s, 0, 0)),
        compiler_params=pltpu.CompilerParams(vmem_limit_bytes=40 * 2**20),
        cost_estimate=pl.CostEstimate(
            flops=8 * steps * GROUP * rows**2 * fields,
            bytes_accessed=4 * (steps * GROUP * rows**2 + 3 * rows * fields),
            transcendentals=0,
        ),
    )(start.reshape(1), a, b, w)


def merge_kernel(mine_ref, low_ref, high_ref, out_ref):
    pairs = low_ref.shape[0]
    out_ref[:pairs] = mine_ref[:pairs] + low_ref[...]
    out_ref[pairs:] = mine_ref[pairs:] + high_ref[...]


def merge(mine, low, high, owners):
    pairs, rows, lanes = mine.shape[0] // owners, *mine.shape[1:]
    whole = pl.BlockSpec((pairs, rows, lanes), lambda m: (m, 0, 0))
    part = pl.BlockSpec((pairs // 2, rows, lanes), lambda m: (m, 0, 0))
    return pl.pallas_call(
        merge_kernel,
        name="merge",
        grid=(owners,),
        out_shape=jax.ShapeDtypeStruct(mine.shape, jnp.float32),
        in_specs=[whole, part, part],
        out_specs=whole,
        compiler_params=pltpu.CompilerParams(vmem_limit_bytes=8 * 2**20),
    )(mine, low, high)


def regroup_kernel(half_ref, arrived_ref, send_ref, own_ref, other_ref, sum_ref):
    pairs, rows, _ = sum_ref.shape
    per_owner = rows // send_ref.shape[0]
    sum_ref[...] = jnp.sum(arrived_ref[...], axis=0)
    for g in range(send_ref.shape[0]):
        for p in range(pairs):
            send_ref[g, p * per_owner : (p + 1) * per_owner] = sum_ref[p, g * per_owner : (g + 1) * per_owner]
    half = half_ref[0]
    for p in range(pairs // 2):
        own_ref[p] = sum_ref[half * (pairs // 2) + p]
        other_ref[p] = sum_ref[(1 - half) * (pairs // 2) + p]


def regroup(half, arrived, parts):
    _, pairs, rows, lanes = arrived.shape
    kept = jax.ShapeDtypeStruct((pairs // 2, rows, lanes), jnp.float32)
    return pl.pallas_call(
        regroup_kernel,
        name="regroup",
        out_shape=(jax.ShapeDtypeStruct((parts, pairs * rows // parts, lanes), jnp.float32), kept, kept),
        in_specs=[pl.BlockSpec(memory_space=pltpu.SMEM)] + in_vmem(1),
        out_specs=tuple(in_vmem(3)),
        scratch_shapes=[pltpu.VMEM((pairs, rows, lanes), jnp.float32)],
        compiler_params=pltpu.CompilerParams(vmem_limit_bytes=8 * 2**20),
    )(half, arrived)


def finish_kernel(own_ref, other_ref, turned_ref, first_ref, second_ref, sum_ref, row_ref):
    pairs, rows, lanes = own_ref.shape
    left = lax.broadcasted_iota(jnp.int32, (rows // 2, lanes), 1) < lanes // 2
    for p in range(pairs):
        sum_ref[p * rows : (p + 1) * rows] = own_ref[p] + other_ref[p]
    for p in range(pairs):
        even = sum_ref[pl.ds(p * rows, rows // 2, stride=2), :]
        odd = sum_ref[pl.ds(p * rows + 1, rows // 2, stride=2), :]
        row_ref[p * rows : p * rows + rows // 2] = jnp.where(left, even, pltpu.roll(odd, lanes // 2, 1))
        row_ref[p * rows + rows // 2 : (p + 1) * rows] = jnp.where(left, pltpu.roll(even, lanes // 2, 1), odd)
    for c in range(rows // 2):
        first_ref[:, c * lanes : (c + 1) * lanes] = row_ref[pl.ds(c, 2 * pairs, stride=rows // 2), :]

    parts, height, _ = turned_ref.shape
    per_owner = second_ref.shape[0]
    pairs = height // per_owner
    for z in range(parts // 2):
        for p in range(pairs):
            c = z * pairs + p
            at = slice(p * per_owner, (p + 1) * per_owner)
            second_ref[:, c * lanes : (c + 1) * lanes] = turned_ref[2 * z, at] + turned_ref[2 * z + 1, at]


def finish(own, other, turned):
    pairs, rows, lanes = own.shape
    out = jax.ShapeDtypeStruct((2 * pairs, rows * lanes // 2), jnp.float32)
    return pl.pallas_call(
        finish_kernel,
        name="finish",
        out_shape=(out, out),
        in_specs=in_vmem(3),
        out_specs=tuple(in_vmem(2)),
        scratch_shapes=[pltpu.VMEM((pairs * rows, lanes), jnp.float32)] * 2,
        compiler_params=pltpu.CompilerParams(vmem_limit_bytes=4 * 2**20),
    )(own, other, turned)


def per_device(vectors):
    blocks, parts = lax.axis_size("vec"), lax.axis_size("field")
    rows = vectors.shape[0]
    scale = 1.0 / math.sqrt(vectors.shape[1] * parts)
    previous = passed_along(vectors, "vec", 1)
    following = passed_along(vectors, "vec", -1)
    here = fetched(vectors)
    peers = parts // 2
    run = rows // peers
    parity = lax.axis_index("field") // 2 % 2
    w = weights(following)

    def sent(part, towards):
        sums = triples(
            (1 - parity) * run + part * (run // 2), previous, here, w, scale, rows // 4 // GROUP, run // 2, 2 * run
        )
        moves = [(2 * z + half, 2 * (towards(z) % peers) + half) for z in range(peers) for half in range(2)]
        return lax.ppermute(sums, "field", moves)

    low = sent(0, lambda z: z ^ 1)
    high = sent(1, lambda z: z + 1 if z % 2 else z - 1)
    mine = triples(parity * run, previous, here, w, scale, rows // 2 // GROUP, run, 2 * run)
    merged = merge(mine, low, high, peers // 2)
    along_z = [[2 * z + half for z in range(q, peers, 2)] for q in range(2) for half in range(2)]
    pieces = merged.reshape(peers // 2, run // 2, rows, 2 * rows)
    arrived = lax.all_to_all(pieces, "field", 0, 0, axis_index_groups=along_z, tiled=True)
    half = (lax.axis_index("field") & 1).reshape(1)
    send, own, other = regroup(half, arrived, parts)
    crossed = [(b * parts + f, (b - 1) % blocks * parts + (f ^ 1)) for b in range(blocks) for f in range(parts)]
    turned = lax.all_to_all(send, "field", split_axis=0, concat_axis=0, tiled=True)
    other = lax.ppermute(other, ("vec", "field"), crossed)
    own = passed_along(own, "vec", -1)
    return finish(own, other, turned)


def solution(mesh):
    placed = (P("vec", "field"),)
    return jax.shard_map(
        per_device,
        mesh=mesh,
        in_specs=placed,
        out_specs=(P(("vec", "field"), None), P(("vec", "field"), None)),
        check_vma=False,
    )
```

```python
import functools
import math

import jax
import jax.numpy as jnp
from jax import lax
from jax.experimental import pallas as pl
from jax.experimental.pallas import tpu as pltpu
from jax.sharding import PartitionSpec as P


GROUP = 16


def passed_along(x, axis, by):
    peers = lax.axis_size(axis)
    return lax.ppermute(x, axis, [(i, (i + by) % peers) for i in range(peers)])


def two_halves(x):
    high = x.astype(jnp.bfloat16)
    return high, (x - high.astype(jnp.float32)).astype(jnp.bfloat16)


def in_vmem(count):
    return [pl.BlockSpec(memory_space=pltpu.VMEM)] * count


def fetch_kernel(parity_ref, in_ref, out_ref, early_ref, late_ref, *, run):
    out_ref[...] = in_ref[...]
    for m in range(early_ref.shape[0] // run):
        at = pl.ds(m * run, run)
        early_ref[at, :] = in_ref[pl.ds(pl.multiple_of(2 * m * run + (1 - parity_ref[0]) * run, run), run), :]
        late_ref[at, :] = in_ref[pl.ds(pl.multiple_of(2 * m * run + parity_ref[0] * run, run), run), :]


def fetched(parity, x, run):
    rows, fields = x.shape
    half = jax.ShapeDtypeStruct((rows // 2, fields), x.dtype)
    return pl.pallas_call(
        functools.partial(fetch_kernel, run=run),
        name="fetch",
        out_shape=(jax.ShapeDtypeStruct(x.shape, x.dtype), half, half),
        in_specs=[pl.BlockSpec(memory_space=pltpu.SMEM)] + in_vmem(1),
        out_specs=tuple(in_vmem(3)),
        compiler_params=pltpu.CompilerParams(vmem_limit_bytes=4 * 2**20),
        cost_estimate=pl.CostEstimate(flops=0, bytes_accessed=3 * x.size * 4, transcendentals=0),
    )(parity.reshape(1), x)


def weights_kernel(c_ref, w_ref):
    w_ref[...] = jnp.concatenate(two_halves(c_ref[...]), 0).T


def weights(c):
    rows, fields = c.shape
    return pl.pallas_call(
        weights_kernel,
        name="weights",
        out_shape=jax.ShapeDtypeStruct((fields, 2 * rows), jnp.bfloat16),
        in_specs=in_vmem(1),
        out_specs=pl.BlockSpec(memory_space=pltpu.VMEM),
        compiler_params=pltpu.CompilerParams(vmem_limit_bytes=8 * 2**20),
        cost_estimate=pl.CostEstimate(flops=c.size, bytes_accessed=8 * c.size, transcendentals=0),
    )(c)


def triple_kernel(scale, start, run, stride, a_ref, b_ref, w_ref, out_ref):
    rows = b_ref.shape[0]
    first_half = lax.broadcasted_iota(jnp.int32, (rows, 2 * rows), 1) < rows
    start = start + pl.program_id(0) * (GROUP // run * stride)
    highs, lows = [], []
    for u in range(GROUP):
        high, low = two_halves(a_ref[pl.ds(start + u // run * stride + u % run, 1), :] * b_ref[...])
        highs.append(high)
        lows.append(low)
    w = w_ref[...]
    r = jnp.dot(jnp.concatenate(highs, 0), w, preferred_element_type=jnp.float32)
    r = r + jnp.dot(jnp.concatenate(lows, 0), w, preferred_element_type=jnp.float32)
    r = (r + pltpu.roll(r, rows, 1)) * scale
    for u in range(GROUP // 2):
        even = r[2 * u * rows : (2 * u + 1) * rows]
        odd = r[(2 * u + 1) * rows : (2 * u + 2) * rows]
        out_ref[u] = jnp.where(first_half, even, odd)


def triples(a, b, w, scale, steps, start, run, stride):
    rows, fields = b.shape
    return pl.pallas_call(
        lambda *refs: triple_kernel(scale, start, run, stride, *refs),
        name="triples",
        grid=(steps,),
        out_shape=jax.ShapeDtypeStruct((steps * GROUP // 2, rows, 2 * rows), jnp.float32),
        in_specs=in_vmem(3),
        out_specs=pl.BlockSpec((GROUP // 2, rows, 2 * rows), lambda s: (s, 0, 0)),
        compiler_params=pltpu.CompilerParams(vmem_limit_bytes=40 * 2**20),
        cost_estimate=pl.CostEstimate(
            flops=8 * steps * GROUP * rows**2 * fields,
            bytes_accessed=4 * (steps * GROUP * rows**2 + 3 * rows * fields),
            transcendentals=0,
        ),
    )(a, b, w)


def merge_kernel(mine_ref, theirs_ref, *refs):
    refs[-1][...] = mine_ref[...] + theirs_ref[...]


def merge(mine, theirs, part, held=None):
    owners, _, pairs, rows, lanes = mine.shape
    block = pl.BlockSpec((owners, 1, pairs, rows, lanes), lambda step: (0, part, 0, 0, 0))
    whole = pl.BlockSpec((owners, 1, pairs, rows, lanes), lambda step: (0, 0, 0, 0, 0))
    more = () if held is None else (held,)
    return pl.pallas_call(
        merge_kernel,
        name="merge",
        grid=(1,),
        out_shape=jax.ShapeDtypeStruct(mine.shape, jnp.float32),
        in_specs=[block, whole] + [pl.BlockSpec(memory_space=pl.ANY)] * len(more),
        out_specs=block,
        input_output_aliases={2: 0} if more else {},
        compiler_params=pltpu.CompilerParams(vmem_limit_bytes=8 * 2**20),
    )(mine, theirs.reshape(owners, 1, pairs, rows, lanes), *more)


def regroup_kernel(half_ref, arrived_ref, send_ref, own_ref, other_ref, sum_ref):
    pairs, rows, _ = sum_ref.shape
    per_owner = rows // send_ref.shape[0]
    sum_ref[...] = jnp.sum(arrived_ref[...], axis=0)
    for g in range(send_ref.shape[0]):
        for p in range(pairs):
            send_ref[g, p * per_owner : (p + 1) * per_owner] = sum_ref[p, g * per_owner : (g + 1) * per_owner]
    half = half_ref[0]
    for p in range(pairs // 2):
        own_ref[p] = sum_ref[half * (pairs // 2) + p]
        other_ref[p] = sum_ref[(1 - half) * (pairs // 2) + p]


def regroup(half, arrived, parts):
    _, pairs, rows, lanes = arrived.shape
    kept = jax.ShapeDtypeStruct((pairs // 2, rows, lanes), jnp.float32)
    return pl.pallas_call(
        regroup_kernel,
        name="regroup",
        out_shape=(jax.ShapeDtypeStruct((parts, pairs * rows // parts, lanes), jnp.float32), kept, kept),
        in_specs=[pl.BlockSpec(memory_space=pltpu.SMEM)] + in_vmem(1),
        out_specs=tuple(in_vmem(3)),
        scratch_shapes=[pltpu.VMEM((pairs, rows, lanes), jnp.float32)],
        compiler_params=pltpu.CompilerParams(vmem_limit_bytes=8 * 2**20),
    )(half, arrived)


def finish_kernel(own_ref, other_ref, turned_ref, first_ref, second_ref, sum_ref, row_ref):
    pairs, rows, lanes = own_ref.shape
    left = lax.broadcasted_iota(jnp.int32, (rows // 2, lanes), 1) < lanes // 2
    for p in range(pairs):
        sum_ref[p * rows : (p + 1) * rows] = own_ref[p] + other_ref[p]
    for p in range(pairs):
        even = sum_ref[pl.ds(p * rows, rows // 2, stride=2), :]
        odd = sum_ref[pl.ds(p * rows + 1, rows // 2, stride=2), :]
        row_ref[p * rows : p * rows + rows // 2] = jnp.where(left, even, pltpu.roll(odd, lanes // 2, 1))
        row_ref[p * rows + rows // 2 : (p + 1) * rows] = jnp.where(left, pltpu.roll(even, lanes // 2, 1), odd)
    for c in range(rows // 2):
        first_ref[:, c * lanes : (c + 1) * lanes] = row_ref[pl.ds(c, 2 * pairs, stride=rows // 2), :]

    parts, height, _ = turned_ref.shape
    per_owner = second_ref.shape[0]
    pairs = height // per_owner
    for z in range(parts // 2):
        for p in range(pairs):
            c = z * pairs + p
            at = slice(p * per_owner, (p + 1) * per_owner)
            second_ref[:, c * lanes : (c + 1) * lanes] = turned_ref[2 * z, at] + turned_ref[2 * z + 1, at]


def finish(own, other, turned):
    pairs, rows, lanes = own.shape
    out = jax.ShapeDtypeStruct((2 * pairs, rows * lanes // 2), jnp.float32)
    return pl.pallas_call(
        finish_kernel,
        name="finish",
        out_shape=(out, out),
        in_specs=in_vmem(3),
        out_specs=tuple(in_vmem(2)),
        scratch_shapes=[pltpu.VMEM((pairs * rows, lanes), jnp.float32)] * 2,
        compiler_params=pltpu.CompilerParams(vmem_limit_bytes=4 * 2**20),
    )(own, other, turned)


def per_device(vectors):
    blocks, parts = lax.axis_size("vec"), lax.axis_size("field")
    rows = vectors.shape[0]
    scale = 1.0 / math.sqrt(vectors.shape[1] * parts)
    peers = parts // 2
    run = rows // peers
    following = passed_along(vectors, "vec", -1)
    here, early, late = fetched(lax.axis_index("field") // 2 % 2, vectors, run)
    early = passed_along(early, "vec", 1)
    late = passed_along(late, "vec", 1)
    w = weights(following)

    def sent(part, towards):
        sums = triples(early, here, w, scale, rows // 4 // GROUP, part * (run // 2), run // 2, run)
        moves = [(2 * z + half, 2 * (towards(z) % peers) + half) for z in range(peers) for half in range(2)]
        return lax.ppermute(sums, "field", moves)

    low = sent(0, lambda z: z ^ 1)
    high = sent(1, lambda z: z + 1 if z % 2 else z - 1)
    mine = triples(late, here, w, scale, rows // 2 // GROUP, 0, run, run)
    mine = mine.reshape(peers // 2, 2, run // 4, rows, 2 * rows)
    merged = merge(mine, high, 1, merge(mine, low, 0))
    along_z = [[2 * z + half for z in range(q, peers, 2)] for q in range(2) for half in range(2)]
    pieces = merged.reshape(peers // 2, run // 2, rows, 2 * rows)
    arrived = lax.all_to_all(pieces, "field", 0, 0, axis_index_groups=along_z, tiled=True)
    half = (lax.axis_index("field") & 1).reshape(1)
    send, own, other = regroup(half, arrived, parts)
    crossed = [(b * parts + f, (b - 1) % blocks * parts + (f ^ 1)) for b in range(blocks) for f in range(parts)]
    turned = lax.all_to_all(send, "field", split_axis=0, concat_axis=0, tiled=True)
    other = lax.ppermute(other, ("vec", "field"), crossed)
    own = passed_along(own, "vec", -1)
    return finish(own, other, turned)


def solution(mesh):
    placed = (P("vec", "field"),)
    return jax.shard_map(
        per_device,
        mesh=mesh,
        in_specs=placed,
        out_specs=(P(("vec", "field"), None), P(("vec", "field"), None)),
        check_vma=False,
    )
```

```python
import functools
import math

import jax
import jax.numpy as jnp
from jax import lax
from jax.experimental import pallas as pl
from jax.experimental.pallas import tpu as pltpu
from jax.sharding import PartitionSpec as P


GROUP = 16
LINE = 8


def passed_along(x, axis, by):
    peers = lax.axis_size(axis)
    return lax.ppermute(x, axis, [(i, (i + by) % peers) for i in range(peers)])


def two_halves(x):
    high = x.astype(jnp.bfloat16)
    return high, (x - high.astype(jnp.float32)).astype(jnp.bfloat16)


def in_vmem(count):
    return [pl.BlockSpec(memory_space=pltpu.VMEM)] * count


def fetch_kernel(in_ref, out_ref):
    out_ref[...] = in_ref[...]


def fetched(x):
    return pl.pallas_call(
        fetch_kernel,
        name="fetch",
        out_shape=jax.ShapeDtypeStruct(x.shape, x.dtype),
        in_specs=in_vmem(1),
        out_specs=pl.BlockSpec(memory_space=pltpu.VMEM),
        compiler_params=pltpu.CompilerParams(vmem_limit_bytes=4 * 2**20),
        cost_estimate=pl.CostEstimate(flops=0, bytes_accessed=2 * x.size * 4, transcendentals=0),
    )(x)


def inputs_kernel(parity_ref, first_ref, last_ref, previous_ref, following_ref, turned_ref, a_ref, w_ref, *, run):
    parity, first, last = parity_ref[0], first_ref[0] == 1, last_ref[0] == 1
    half = a_ref.shape[0] // 2
    for m in range(half // run):
        for at, which in ((m * run, 1 - parity), (half + m * run, parity)):
            rows = pl.ds(pl.multiple_of((2 * m + which) * run, run), run)
            a_ref[at : at + run, :] = jnp.where(first, turned_ref[rows, :], previous_ref[rows, :])
    c = jnp.where(last, turned_ref[...], following_ref[...])
    w_ref[...] = jnp.concatenate(two_halves(c), 0).T


def inputs(place, previous, following, turned, run):
    rows, fields = previous.shape
    return pl.pallas_call(
        functools.partial(inputs_kernel, run=run),
        name="inputs",
        out_shape=(
            jax.ShapeDtypeStruct(previous.shape, jnp.float32),
            jax.ShapeDtypeStruct((fields, 2 * rows), jnp.bfloat16),
        ),
        in_specs=[pl.BlockSpec(memory_space=pltpu.SMEM)] * 3 + in_vmem(3),
        out_specs=tuple(in_vmem(2)),
        compiler_params=pltpu.CompilerParams(vmem_limit_bytes=8 * 2**20),
        cost_estimate=pl.CostEstimate(flops=previous.size, bytes_accessed=20 * previous.size, transcendentals=0),
    )(*place, previous, following, turned)


def triple_kernel(scale, start, run, stride, a_ref, b_ref, w_ref, out_ref):
    rows = b_ref.shape[0]
    first_half = lax.broadcasted_iota(jnp.int32, (rows, 2 * rows), 1) < rows
    start = start + pl.program_id(0) * (GROUP // run * stride)
    highs, lows = [], []
    for u in range(GROUP):
        high, low = two_halves(a_ref[pl.ds(start + u // run * stride + u % run, 1), :] * b_ref[...])
        highs.append(high)
        lows.append(low)
    w = w_ref[...]
    r = jnp.dot(jnp.concatenate(highs, 0), w, preferred_element_type=jnp.float32)
    r = r + jnp.dot(jnp.concatenate(lows, 0), w, preferred_element_type=jnp.float32)
    r = (r + pltpu.roll(r, rows, 1)) * scale
    for u in range(GROUP // 2):
        even = r[2 * u * rows : (2 * u + 1) * rows]
        odd = r[(2 * u + 1) * rows : (2 * u + 2) * rows]
        out_ref[u] = jnp.where(first_half, even, odd)


def triples(a, b, w, scale, steps, start, run, stride):
    rows, fields = b.shape
    return pl.pallas_call(
        lambda *refs: triple_kernel(scale, start, run, stride, *refs),
        name="triples",
        grid=(steps,),
        out_shape=jax.ShapeDtypeStruct((steps * GROUP // 2, rows, 2 * rows), jnp.float32),
        in_specs=in_vmem(3),
        out_specs=pl.BlockSpec((GROUP // 2, rows, 2 * rows), lambda s: (s, 0, 0)),
        compiler_params=pltpu.CompilerParams(vmem_limit_bytes=40 * 2**20),
        cost_estimate=pl.CostEstimate(
            flops=8 * steps * GROUP * rows**2 * fields,
            bytes_accessed=4 * (steps * GROUP * rows**2 + 3 * rows * fields),
            transcendentals=0,
        ),
    )(a, b, w)


def merge_kernel(mine_ref, theirs_ref, *refs):
    refs[-1][...] = mine_ref[...] + theirs_ref[...]


def merge(mine, theirs, part, held=None):
    owners, _, pairs, rows, lanes = mine.shape
    block = pl.BlockSpec((owners, 1, pairs, rows, lanes), lambda step: (0, part, 0, 0, 0))
    whole = pl.BlockSpec((owners, 1, pairs, rows, lanes), lambda step: (0, 0, 0, 0, 0))
    more = () if held is None else (held,)
    return pl.pallas_call(
        merge_kernel,
        name="merge",
        grid=(1,),
        out_shape=jax.ShapeDtypeStruct(mine.shape, jnp.float32),
        in_specs=[block, whole] + [pl.BlockSpec(memory_space=pl.ANY)] * len(more),
        out_specs=block,
        input_output_aliases={2: 0} if more else {},
        compiler_params=pltpu.CompilerParams(vmem_limit_bytes=8 * 2**20),
    )(mine, theirs.reshape(owners, 1, pairs, rows, lanes), *more)


def regroup_kernel(half_ref, arrived_ref, send_ref, own_ref, other_ref, sum_ref):
    pairs, rows, _ = sum_ref.shape
    per_owner = rows // send_ref.shape[0]
    sum_ref[...] = jnp.sum(arrived_ref[...], axis=0)
    for g in range(send_ref.shape[0]):
        for p in range(pairs):
            send_ref[g, p * per_owner : (p + 1) * per_owner] = sum_ref[p, g * per_owner : (g + 1) * per_owner]
    half = half_ref[0]
    for p in range(pairs // 2):
        own_ref[p] = sum_ref[half * (pairs // 2) + p]
        other_ref[p] = sum_ref[(1 - half) * (pairs // 2) + p]


def regroup(half, arrived, parts):
    _, pairs, rows, lanes = arrived.shape
    kept = jax.ShapeDtypeStruct((pairs // 2, rows, lanes), jnp.float32)
    return pl.pallas_call(
        regroup_kernel,
        name="regroup",
        out_shape=(jax.ShapeDtypeStruct((parts, pairs * rows // parts, lanes), jnp.float32), kept, kept),
        in_specs=[pl.BlockSpec(memory_space=pltpu.SMEM)] + in_vmem(1),
        out_specs=tuple(in_vmem(3)),
        scratch_shapes=[pltpu.VMEM((pairs, rows, lanes), jnp.float32)],
        compiler_params=pltpu.CompilerParams(vmem_limit_bytes=8 * 2**20),
    )(half, arrived)


def finish_kernel(own_ref, other_ref, turned_ref, first_ref, second_ref, sum_ref, row_ref):
    pairs, rows, lanes = own_ref.shape
    left = lax.broadcasted_iota(jnp.int32, (rows // 2, lanes), 1) < lanes // 2
    for p in range(pairs):
        sum_ref[p * rows : (p + 1) * rows] = own_ref[p] + other_ref[p]
    for p in range(pairs):
        even = sum_ref[pl.ds(p * rows, rows // 2, stride=2), :]
        odd = sum_ref[pl.ds(p * rows + 1, rows // 2, stride=2), :]
        row_ref[p * rows : p * rows + rows // 2] = jnp.where(left, even, pltpu.roll(odd, lanes // 2, 1))
        row_ref[p * rows + rows // 2 : (p + 1) * rows] = jnp.where(left, pltpu.roll(even, lanes // 2, 1), odd)
    for c in range(rows // 2):
        first_ref[:, c * lanes : (c + 1) * lanes] = row_ref[pl.ds(c, 2 * pairs, stride=rows // 2), :]

    parts, height, _ = turned_ref.shape
    per_owner = second_ref.shape[0]
    pairs = height // per_owner
    for z in range(parts // 2):
        for p in range(pairs):
            c = z * pairs + p
            at = slice(p * per_owner, (p + 1) * per_owner)
            second_ref[:, c * lanes : (c + 1) * lanes] = turned_ref[2 * z, at] + turned_ref[2 * z + 1, at]


def finish(own, other, turned):
    pairs, rows, lanes = own.shape
    out = jax.ShapeDtypeStruct((2 * pairs, rows * lanes // 2), jnp.float32)
    return pl.pallas_call(
        finish_kernel,
        name="finish",
        out_shape=(out, out),
        in_specs=in_vmem(3),
        out_specs=tuple(in_vmem(2)),
        scratch_shapes=[pltpu.VMEM((pairs * rows, lanes), jnp.float32)] * 2,
        compiler_params=pltpu.CompilerParams(vmem_limit_bytes=4 * 2**20),
    )(own, other, turned)


def per_device(vectors):
    blocks, parts = lax.axis_size("vec"), lax.axis_size("field")
    rows = vectors.shape[0]
    scale = 1.0 / math.sqrt(vectors.shape[1] * parts)
    peers = parts // 2
    run = rows // peers
    line = LINE if blocks % LINE == 0 else blocks
    ends = [((b - 1) % blocks, b) for b in range(0, blocks, line)]
    inner = [(b - 1, b) for b in range(blocks) if b % line]
    turned = lax.ppermute(vectors, "vec", ends + [(b, a) for a, b in ends])
    here = fetched(vectors)
    following = lax.ppermute(vectors, "vec", [(b, a) for a, b in inner])
    previous = lax.ppermute(vectors, "vec", inner)
    spot = lax.rem(lax.axis_index("vec"), line)
    parity = lax.axis_index("field") // 2 & 1
    place = [x.astype(jnp.int32).reshape(1) for x in (parity, spot == 0, spot == line - 1)]
    a, w = inputs(place, previous, following, turned, run)

    def sent(part, towards):
        sums = triples(a, here, w, scale, rows // 4 // GROUP, part * (run // 2), run // 2, run)
        moves = [(2 * z + half, 2 * (towards(z) % peers) + half) for z in range(peers) for half in range(2)]
        return lax.ppermute(sums, "field", moves)

    low = sent(0, lambda z: z ^ 1)
    high = sent(1, lambda z: z + 1 if z % 2 else z - 1)
    mine = triples(a, here, w, scale, rows // 2 // GROUP, rows // 2, run, run)
    mine = mine.reshape(peers // 2, 2, run // 4, rows, 2 * rows)
    merged = merge(mine, high, 1, merge(mine, low, 0))
    along_z = [[2 * z + half for z in range(q, peers, 2)] for q in range(2) for half in range(2)]
    pieces = merged.reshape(peers // 2, run // 2, rows, 2 * rows)
    arrived = lax.all_to_all(pieces, "field", 0, 0, axis_index_groups=along_z, tiled=True)
    half = (lax.axis_index("field") & 1).reshape(1)
    send, own, other = regroup(half, arrived, parts)
    crossed = [(b * parts + f, (b - 1) % blocks * parts + (f ^ 1)) for b in range(blocks) for f in range(parts)]
    turned = lax.all_to_all(send, "field", split_axis=0, concat_axis=0, tiled=True)
    other = lax.ppermute(other, ("vec", "field"), crossed)
    own = passed_along(own, "vec", -1)
    return finish(own, other, turned)


def solution(mesh):
    placed = (P("vec", "field"),)
    return jax.shard_map(
        per_device,
        mesh=mesh,
        in_specs=placed,
        out_specs=(P(("vec", "field"), None), P(("vec", "field"), None)),
        check_vma=False,
    )
```

```python
import functools
import math

import jax
import jax.numpy as jnp
from jax import lax
from jax.experimental import pallas as pl
from jax.experimental.pallas import tpu as pltpu
from jax.sharding import PartitionSpec as P


GROUP = 16
LINE = 8


def passed_along(x, axis, by):
    peers = lax.axis_size(axis)
    return lax.ppermute(x, axis, [(i, (i + by) % peers) for i in range(peers)])


def two_halves(x):
    high = x.astype(jnp.bfloat16)
    return high, (x - high.astype(jnp.float32)).astype(jnp.bfloat16)


def in_vmem(count):
    return [pl.BlockSpec(memory_space=pltpu.VMEM)] * count


def fetch_kernel(in_ref, out_ref):
    out_ref[...] = in_ref[...]


def fetched(x):
    return pl.pallas_call(
        fetch_kernel,
        name="fetch",
        out_shape=jax.ShapeDtypeStruct(x.shape, x.dtype),
        in_specs=in_vmem(1),
        out_specs=pl.BlockSpec(memory_space=pltpu.VMEM),
        compiler_params=pltpu.CompilerParams(vmem_limit_bytes=4 * 2**20),
        cost_estimate=pl.CostEstimate(flops=0, bytes_accessed=2 * x.size * 4, transcendentals=0),
    )(x)


def inputs_kernel(parity_ref, first_ref, last_ref, previous_ref, following_ref, turned_ref, a_ref, w_ref, *, run):
    parity, first, last = parity_ref[0], first_ref[0] == 1, last_ref[0] == 1
    half = a_ref.shape[0] // 2
    for m in range(half // run):
        for at, which in ((m * run, 1 - parity), (half + m * run, parity)):
            rows = pl.ds(pl.multiple_of((2 * m + which) * run, run), run)
            a_ref[at : at + run, :] = jnp.where(first, turned_ref[rows, :], previous_ref[rows, :])
    c = jnp.where(last, turned_ref[...], following_ref[...])
    w_ref[...] = jnp.concatenate(two_halves(c), 0).T


def inputs(place, previous, following, turned, run):
    rows, fields = previous.shape
    return pl.pallas_call(
        functools.partial(inputs_kernel, run=run),
        name="inputs",
        out_shape=(
            jax.ShapeDtypeStruct(previous.shape, jnp.float32),
            jax.ShapeDtypeStruct((fields, 2 * rows), jnp.bfloat16),
        ),
        in_specs=[pl.BlockSpec(memory_space=pltpu.SMEM)] * 3 + in_vmem(3),
        out_specs=tuple(in_vmem(2)),
        compiler_params=pltpu.CompilerParams(vmem_limit_bytes=8 * 2**20),
        cost_estimate=pl.CostEstimate(flops=previous.size, bytes_accessed=20 * previous.size, transcendentals=0),
    )(*place, previous, following, turned)


def triple_kernel(scale, start, run, stride, a_ref, b_ref, w_ref, out_ref):
    rows = b_ref.shape[0]
    first_half = lax.broadcasted_iota(jnp.int32, (rows, 2 * rows), 1) < rows
    start = start + pl.program_id(0) * (GROUP // run * stride)
    highs, lows = [], []
    for u in range(GROUP):
        high, low = two_halves(a_ref[pl.ds(start + u // run * stride + u % run, 1), :] * b_ref[...])
        highs.append(high)
        lows.append(low)
    w = w_ref[...]
    r = jnp.dot(jnp.concatenate(highs, 0), w, preferred_element_type=jnp.float32)
    r = r + jnp.dot(jnp.concatenate(lows, 0), w, preferred_element_type=jnp.float32)
    r = (r + pltpu.roll(r, rows, 1)) * scale
    for u in range(GROUP // 2):
        even = r[2 * u * rows : (2 * u + 1) * rows]
        odd = r[(2 * u + 1) * rows : (2 * u + 2) * rows]
        out_ref[u] = jnp.where(first_half, even, odd)


def triples(a, b, w, scale, steps, start, run, stride):
    rows, fields = b.shape
    return pl.pallas_call(
        lambda *refs: triple_kernel(scale, start, run, stride, *refs),
        name="triples",
        grid=(steps,),
        out_shape=jax.ShapeDtypeStruct((steps * GROUP // 2, rows, 2 * rows), jnp.float32),
        in_specs=in_vmem(3),
        out_specs=pl.BlockSpec((GROUP // 2, rows, 2 * rows), lambda s: (s, 0, 0)),
        compiler_params=pltpu.CompilerParams(vmem_limit_bytes=40 * 2**20),
        cost_estimate=pl.CostEstimate(
            flops=8 * steps * GROUP * rows**2 * fields,
            bytes_accessed=4 * (steps * GROUP * rows**2 + 3 * rows * fields),
            transcendentals=0,
        ),
    )(a, b, w)


def merge_kernel(mine_ref, theirs_ref, *refs):
    refs[-1][...] = mine_ref[...] + theirs_ref[...]


def merge(mine, theirs, part, held=None):
    owners, _, pairs, rows, lanes = mine.shape
    block = pl.BlockSpec((owners, 1, pairs, rows, lanes), lambda step: (0, part, 0, 0, 0))
    whole = pl.BlockSpec((owners, 1, pairs, rows, lanes), lambda step: (0, 0, 0, 0, 0))
    more = () if held is None else (held,)
    return pl.pallas_call(
        merge_kernel,
        name="merge",
        grid=(1,),
        out_shape=jax.ShapeDtypeStruct(mine.shape, jnp.float32),
        in_specs=[block, whole] + [pl.BlockSpec(memory_space=pl.ANY)] * len(more),
        out_specs=block,
        input_output_aliases={2: 0} if more else {},
        compiler_params=pltpu.CompilerParams(vmem_limit_bytes=8 * 2**20),
    )(mine, theirs.reshape(owners, 1, pairs, rows, lanes), *more)


def regroup_kernel(arrived_ref, send_ref, own_ref):
    pairs, rows, _ = own_ref.shape
    per_owner = rows // send_ref.shape[0]
    own_ref[...] = jnp.sum(arrived_ref[...], axis=0)
    for g in range(send_ref.shape[0]):
        for p in range(pairs):
            send_ref[g, p * per_owner : (p + 1) * per_owner] = own_ref[p, g * per_owner : (g + 1) * per_owner]


def regroup(arrived, parts):
    _, pairs, rows, lanes = arrived.shape
    return pl.pallas_call(
        regroup_kernel,
        name="regroup",
        out_shape=(
            jax.ShapeDtypeStruct((parts, pairs * rows // parts, lanes), jnp.float32),
            jax.ShapeDtypeStruct((pairs, rows, lanes), jnp.float32),
        ),
        in_specs=in_vmem(1),
        out_specs=tuple(in_vmem(2)),
        compiler_params=pltpu.CompilerParams(vmem_limit_bytes=8 * 2**20),
    )(arrived)


def finish_kernel(own_ref, turned_ref, first_ref, second_ref, sum_ref, row_ref):
    pairs, rows, lanes = own_ref.shape
    left = lax.broadcasted_iota(jnp.int32, (rows // 2, lanes), 1) < lanes // 2
    for p in range(pairs):
        sum_ref[p * rows : (p + 1) * rows] = own_ref[p]
    for p in range(pairs):
        even = sum_ref[pl.ds(p * rows, rows // 2, stride=2), :]
        odd = sum_ref[pl.ds(p * rows + 1, rows // 2, stride=2), :]
        row_ref[p * rows : p * rows + rows // 2] = jnp.where(left, even, pltpu.roll(odd, lanes // 2, 1))
        row_ref[p * rows + rows // 2 : (p + 1) * rows] = jnp.where(left, pltpu.roll(even, lanes // 2, 1), odd)
    for c in range(rows // 2):
        first_ref[:, c * lanes : (c + 1) * lanes] = row_ref[pl.ds(c, 2 * pairs, stride=rows // 2), :]

    per_owner = second_ref.shape[0]
    for f in range(turned_ref.shape[0]):
        for p in range(pairs):
            c = f * pairs + p
            second_ref[:, c * lanes : (c + 1) * lanes] = turned_ref[f, p * per_owner : (p + 1) * per_owner]


def finish(own, turned):
    pairs, rows, lanes = own.shape
    out = jax.ShapeDtypeStruct((2 * pairs, rows * lanes // 2), jnp.float32)
    return pl.pallas_call(
        finish_kernel,
        name="finish",
        out_shape=(out, out),
        in_specs=in_vmem(2),
        out_specs=tuple(in_vmem(2)),
        scratch_shapes=[pltpu.VMEM((pairs * rows, lanes), jnp.float32)] * 2,
        compiler_params=pltpu.CompilerParams(vmem_limit_bytes=4 * 2**20),
    )(own, turned)


def per_device(vectors):
    blocks, parts = lax.axis_size("vec"), lax.axis_size("field")
    rows = vectors.shape[0]
    scale = 1.0 / math.sqrt(vectors.shape[1] * parts)
    peers = parts // 2
    run = rows // peers
    line = LINE if blocks % LINE == 0 else blocks
    ends = [((b - 1) % blocks, b) for b in range(0, blocks, line)]
    inner = [(b - 1, b) for b in range(blocks) if b % line]
    turned = lax.ppermute(vectors, "vec", ends + [(b, a) for a, b in ends])
    here = fetched(vectors)
    following = lax.ppermute(vectors, "vec", [(b, a) for a, b in inner])
    previous = lax.ppermute(vectors, "vec", inner)
    spot = lax.rem(lax.axis_index("vec"), line)
    parity = lax.axis_index("field") // 2 & 1
    place = [x.astype(jnp.int32).reshape(1) for x in (parity, spot == 0, spot == line - 1)]
    a, w = inputs(place, previous, following, turned, run)

    def sent(part, towards):
        sums = triples(a, here, w, scale, rows // 4 // GROUP, part * (run // 2), run // 2, run)
        moves = [(2 * z + half, 2 * (towards(z) % peers) + half) for z in range(peers) for half in range(2)]
        return lax.ppermute(sums, "field", moves)

    low = sent(0, lambda z: z ^ 1)
    high = sent(1, lambda z: z + 1 if z % 2 else z - 1)
    mine = triples(a, here, w, scale, rows // 2 // GROUP, rows // 2, run, run)
    mine = mine.reshape(peers // 2, 2, run // 4, rows, 2 * rows)
    merged = merge(mine, high, 1, merge(mine, low, 0))
    alike = [[2 * z + half for z in range(q, peers, 2) for half in range(2)] for q in range(2)]
    pieces = merged.reshape(peers, run // 4, rows, 2 * rows)
    arrived = lax.all_to_all(pieces, "field", 0, 0, axis_index_groups=alike, tiled=True)
    send, own = regroup(arrived, parts)
    turned = lax.all_to_all(send, "field", split_axis=0, concat_axis=0, tiled=True)
    own = passed_along(own, "vec", -1)
    return finish(own, turned)


def solution(mesh):
    placed = (P("vec", "field"),)
    return jax.shard_map(
        per_device,
        mesh=mesh,
        in_specs=placed,
        out_specs=(P(("vec", "field"), None), P(("vec", "field"), None)),
        check_vma=False,
    )
```

```python
import functools
import math

import jax
import jax.numpy as jnp
from jax import lax
from jax.experimental import pallas as pl
from jax.experimental.pallas import tpu as pltpu
from jax.sharding import PartitionSpec as P


GROUP = 16
LINE = 8


def passed_along(x, axis, by):
    peers = lax.axis_size(axis)
    return lax.ppermute(x, axis, [(i, (i + by) % peers) for i in range(peers)])


def two_halves(x):
    high = x.astype(jnp.bfloat16)
    return high, (x - high.astype(jnp.float32)).astype(jnp.bfloat16)


def in_vmem(count):
    return [pl.BlockSpec(memory_space=pltpu.VMEM)] * count


def fetch_kernel(in_ref, out_ref):
    out_ref[...] = in_ref[...]


def fetched(x):
    return pl.pallas_call(
        fetch_kernel,
        name="fetch",
        out_shape=jax.ShapeDtypeStruct(x.shape, x.dtype),
        in_specs=in_vmem(1),
        out_specs=pl.BlockSpec(memory_space=pltpu.VMEM),
        compiler_params=pltpu.CompilerParams(vmem_limit_bytes=4 * 2**20),
        cost_estimate=pl.CostEstimate(flops=0, bytes_accessed=2 * x.size * 4, transcendentals=0),
    )(x)


def inputs_kernel(parity_ref, first_ref, last_ref, previous_ref, following_ref, turned_ref, a_ref, w_ref, *, run):
    parity, first, last = parity_ref[0], first_ref[0] == 1, last_ref[0] == 1
    half = a_ref.shape[0] // 2
    for m in range(half // run):
        for at, which in ((m * run, 1 - parity), (half + m * run, parity)):
            rows = pl.ds(pl.multiple_of((2 * m + which) * run, run), run)
            a_ref[at : at + run, :] = jnp.where(first, turned_ref[rows, :], previous_ref[rows, :])
    c = jnp.where(last, turned_ref[...], following_ref[...])
    w_ref[...] = jnp.concatenate(two_halves(c), 0).T


def inputs(place, previous, following, turned, run):
    rows, fields = previous.shape
    return pl.pallas_call(
        functools.partial(inputs_kernel, run=run),
        name="inputs",
        out_shape=(
            jax.ShapeDtypeStruct(previous.shape, jnp.float32),
            jax.ShapeDtypeStruct((fields, 2 * rows), jnp.bfloat16),
        ),
        in_specs=[pl.BlockSpec(memory_space=pltpu.SMEM)] * 3 + in_vmem(3),
        out_specs=tuple(in_vmem(2)),
        compiler_params=pltpu.CompilerParams(vmem_limit_bytes=8 * 2**20),
        cost_estimate=pl.CostEstimate(flops=previous.size, bytes_accessed=20 * previous.size, transcendentals=0),
    )(*place, previous, following, turned)


def triple_kernel(scale, start, run, stride, a_ref, b_ref, w_ref, out_ref):
    rows = b_ref.shape[0]
    first_half = lax.broadcasted_iota(jnp.int32, (rows, 2 * rows), 1) < rows
    start = start + pl.program_id(0) * (GROUP // run * stride)
    highs, lows = [], []
    for u in range(GROUP):
        high, low = two_halves(a_ref[pl.ds(start + u // run * stride + u % run, 1), :] * b_ref[...])
        highs.append(high)
        lows.append(low)
    w = w_ref[...]
    r = jnp.dot(jnp.concatenate(highs, 0), w, preferred_element_type=jnp.float32)
    r = r + jnp.dot(jnp.concatenate(lows, 0), w, preferred_element_type=jnp.float32)
    r = (r + pltpu.roll(r, rows, 1)) * scale
    for u in range(GROUP // 2):
        even = r[2 * u * rows : (2 * u + 1) * rows]
        odd = r[(2 * u + 1) * rows : (2 * u + 2) * rows]
        out_ref[u] = jnp.where(first_half, even, odd)


def triples(a, b, w, scale, steps, start, run, stride):
    rows, fields = b.shape
    return pl.pallas_call(
        lambda *refs: triple_kernel(scale, start, run, stride, *refs),
        name="triples",
        grid=(steps,),
        out_shape=jax.ShapeDtypeStruct((steps * GROUP // 2, rows, 2 * rows), jnp.float32),
        in_specs=in_vmem(3),
        out_specs=pl.BlockSpec((GROUP // 2, rows, 2 * rows), lambda s: (s, 0, 0)),
        compiler_params=pltpu.CompilerParams(vmem_limit_bytes=40 * 2**20),
        cost_estimate=pl.CostEstimate(
            flops=8 * steps * GROUP * rows**2 * fields,
            bytes_accessed=4 * (steps * GROUP * rows**2 + 3 * rows * fields),
            transcendentals=0,
        ),
    )(a, b, w)


def merge_kernel(mine_ref, theirs_ref, *refs):
    refs[-1][...] = mine_ref[...] + theirs_ref[...]


def merge(mine, theirs, part, held=None):
    owners, _, pairs, rows, lanes = mine.shape
    block = pl.BlockSpec((owners, 1, pairs, rows, lanes), lambda step: (0, part, 0, 0, 0))
    whole = pl.BlockSpec((owners, 1, pairs, rows, lanes), lambda step: (0, 0, 0, 0, 0))
    more = () if held is None else (held,)
    return pl.pallas_call(
        merge_kernel,
        name="merge",
        grid=(1,),
        out_shape=jax.ShapeDtypeStruct(mine.shape, jnp.float32),
        in_specs=[block, whole] + [pl.BlockSpec(memory_space=pl.ANY)] * len(more),
        out_specs=block,
        input_output_aliases={2: 0} if more else {},
        compiler_params=pltpu.CompilerParams(vmem_limit_bytes=8 * 2**20),
    )(mine, theirs.reshape(owners, 1, pairs, rows, lanes), *more)


def regroup_kernel(arrived_ref, send_ref, own_ref, other_ref, sum_ref):
    pairs, rows, _ = sum_ref.shape
    per_owner = rows // send_ref.shape[0]
    sum_ref[...] = jnp.sum(arrived_ref[...], axis=0)
    for g in range(send_ref.shape[0]):
        for p in range(pairs):
            send_ref[g, p * per_owner : (p + 1) * per_owner] = sum_ref[p, g * per_owner : (g + 1) * per_owner]
    half = lax.rem(lax.axis_index("field"), 2)
    for p in range(pairs // 2):
        own_ref[p] = sum_ref[half * (pairs // 2) + p]
        other_ref[p] = sum_ref[(1 - half) * (pairs // 2) + p]


def regroup(arrived, parts):
    _, pairs, rows, lanes = arrived.shape
    kept = jax.ShapeDtypeStruct((pairs // 2, rows, lanes), jnp.float32)
    return pl.pallas_call(
        regroup_kernel,
        name="regroup",
        out_shape=(jax.ShapeDtypeStruct((parts, pairs * rows // parts, lanes), jnp.float32), kept, kept),
        in_specs=in_vmem(1),
        out_specs=tuple(in_vmem(3)),
        scratch_shapes=[pltpu.VMEM((pairs, rows, lanes), jnp.float32)],
        compiler_params=pltpu.CompilerParams(vmem_limit_bytes=8 * 2**20),
    )(arrived)


def finish_kernel(own_ref, other_ref, turned_ref, first_ref, second_ref, sum_ref, row_ref):
    pairs, rows, lanes = own_ref.shape
    left = lax.broadcasted_iota(jnp.int32, (rows // 2, lanes), 1) < lanes // 2
    for p in range(pairs):
        sum_ref[p * rows : (p + 1) * rows] = own_ref[p] + other_ref[p]
    for p in range(pairs):
        even = sum_ref[pl.ds(p * rows, rows // 2, stride=2), :]
        odd = sum_ref[pl.ds(p * rows + 1, rows // 2, stride=2), :]
        row_ref[p * rows : p * rows + rows // 2] = jnp.where(left, even, pltpu.roll(odd, lanes // 2, 1))
        row_ref[p * rows + rows // 2 : (p + 1) * rows] = jnp.where(left, pltpu.roll(even, lanes // 2, 1), odd)
    for c in range(rows // 2):
        first_ref[:, c * lanes : (c + 1) * lanes] = row_ref[pl.ds(c, 2 * pairs, stride=rows // 2), :]

    parts, height, _ = turned_ref.shape
    per_owner = second_ref.shape[0]
    pairs = height // per_owner
    for z in range(parts // 2):
        for p in range(pairs):
            c = z * pairs + p
            at = slice(p * per_owner, (p + 1) * per_owner)
            second_ref[:, c * lanes : (c + 1) * lanes] = turned_ref[2 * z, at] + turned_ref[2 * z + 1, at]


def finish(own, other, turned):
    pairs, rows, lanes = own.shape
    out = jax.ShapeDtypeStruct((2 * pairs, rows * lanes // 2), jnp.float32)
    return pl.pallas_call(
        finish_kernel,
        name="finish",
        out_shape=(out, out),
        in_specs=in_vmem(3),
        out_specs=tuple(in_vmem(2)),
        scratch_shapes=[pltpu.VMEM((pairs * rows, lanes), jnp.float32)] * 2,
        compiler_params=pltpu.CompilerParams(vmem_limit_bytes=4 * 2**20),
    )(own, other, turned)


def per_device(vectors):
    blocks, parts = lax.axis_size("vec"), lax.axis_size("field")
    rows = vectors.shape[0]
    scale = 1.0 / math.sqrt(vectors.shape[1] * parts)
    peers = parts // 2
    run = rows // peers
    line = LINE if blocks % LINE == 0 else blocks
    ends = [((b - 1) % blocks, b) for b in range(0, blocks, line)]
    inner = [(b - 1, b) for b in range(blocks) if b % line]
    turned = lax.ppermute(vectors, "vec", ends + [(b, a) for a, b in ends])
    here = fetched(vectors)
    following = lax.ppermute(vectors, "vec", [(b, a) for a, b in inner])
    previous = lax.ppermute(vectors, "vec", inner)
    spot = lax.rem(lax.axis_index("vec"), line)
    parity = lax.axis_index("field") // 2 & 1
    place = [x.astype(jnp.int32).reshape(1) for x in (parity, spot == 0, spot == line - 1)]
    a, w = inputs(place, previous, following, turned, run)

    def sent(part, towards):
        sums = triples(a, here, w, scale, rows // 4 // GROUP, part * (run // 2), run // 2, run)
        moves = [(2 * z + half, 2 * (towards(z) % peers) + half) for z in range(peers) for half in range(2)]
        return lax.ppermute(sums, "field", moves)

    low = sent(0, lambda z: z ^ 1)
    high = sent(1, lambda z: z + 1 if z % 2 else z - 1)
    mine = triples(a, here, w, scale, rows // 2 // GROUP, rows // 2, run, run)
    mine = mine.reshape(peers // 2, 2, run // 4, rows, 2 * rows)
    merged = merge(mine, high, 1, merge(mine, low, 0))
    along_z = [[2 * z + half for z in range(q, peers, 2)] for q in range(2) for half in range(2)]
    pieces = merged.reshape(peers // 2, run // 2, rows, 2 * rows)
    arrived = lax.all_to_all(pieces, "field", 0, 0, axis_index_groups=along_z, tiled=True)
    send, own, other = regroup(arrived, parts)
    crossed = [(b * parts + f, (b - 1) % blocks * parts + (f ^ 1)) for b in range(blocks) for f in range(parts)]
    turned = lax.all_to_all(send, "field", split_axis=0, concat_axis=0, tiled=True)
    other = lax.ppermute(other, ("vec", "field"), crossed)
    own = passed_along(own, "vec", -1)
    return finish(own, other, turned)


def solution(mesh):
    placed = (P("vec", "field"),)
    return jax.shard_map(
        per_device,
        mesh=mesh,
        in_specs=placed,
        out_specs=(P(("vec", "field"), None), P(("vec", "field"), None)),
        check_vma=False,
    )
```

```python
import math

import jax
import jax.numpy as jnp
from jax import lax
from jax.experimental import pallas as pl
from jax.experimental.pallas import tpu as pltpu
from jax.sharding import PartitionSpec as P


GROUP = 32
LINE = 8


def passed_along(x, axis, by):
    peers = lax.axis_size(axis)
    return lax.ppermute(x, axis, [(i, (i + by) % peers) for i in range(peers)])


def two_halves(x):
    high = x.astype(jnp.bfloat16)
    return high, (x - high.astype(jnp.float32)).astype(jnp.bfloat16)


def in_vmem(count):
    return [pl.BlockSpec(memory_space=pltpu.VMEM)] * count


def fetch_kernel(in_ref, out_ref):
    out_ref[...] = in_ref[...]


def fetched(x):
    return pl.pallas_call(
        fetch_kernel,
        name="fetch",
        out_shape=jax.ShapeDtypeStruct(x.shape, x.dtype),
        in_specs=in_vmem(1),
        out_specs=pl.BlockSpec(memory_space=pltpu.VMEM),
        compiler_params=pltpu.CompilerParams(vmem_limit_bytes=4 * 2**20),
        cost_estimate=pl.CostEstimate(flops=0, bytes_accessed=2 * x.size * 4, transcendentals=0),
    )(x)


def inputs_kernel(first_ref, last_ref, previous_ref, following_ref, turned_ref, a_ref, w_ref):
    a_ref[...] = jnp.where(first_ref[0] == 1, turned_ref[...], previous_ref[...])
    c = jnp.where(last_ref[0] == 1, turned_ref[...], following_ref[...])
    w_ref[...] = jnp.concatenate(two_halves(c), 0).T


def inputs(place, previous, following, turned):
    rows, fields = previous.shape
    return pl.pallas_call(
        inputs_kernel,
        name="inputs",
        out_shape=(
            jax.ShapeDtypeStruct(previous.shape, jnp.float32),
            jax.ShapeDtypeStruct((fields, 2 * rows), jnp.bfloat16),
        ),
        in_specs=[pl.BlockSpec(memory_space=pltpu.SMEM)] * 2 + in_vmem(3),
        out_specs=tuple(in_vmem(2)),
        compiler_params=pltpu.CompilerParams(vmem_limit_bytes=8 * 2**20),
        cost_estimate=pl.CostEstimate(flops=previous.size, bytes_accessed=20 * previous.size, transcendentals=0),
    )(*place, previous, following, turned)


def triple_kernel(scale, a_ref, b_ref, w_ref, out_ref):
    rows = b_ref.shape[0]
    first_half = lax.broadcasted_iota(jnp.int32, (rows, 2 * rows), 1) < rows

    def step(g, carry):
        highs, lows = [], []
        for u in range(GROUP):
            high, low = two_halves(a_ref[pl.ds(g * GROUP + u, 1), :] * b_ref[...])
            highs.append(high)
            lows.append(low)
        w = w_ref[...]
        r = jnp.dot(jnp.concatenate(highs, 0), w, preferred_element_type=jnp.float32)
        r = r + jnp.dot(jnp.concatenate(lows, 0), w, preferred_element_type=jnp.float32)
        r = (r + pltpu.roll(r, rows, 1)) * scale
        for u in range(GROUP // 2):
            even = r[2 * u * rows : (2 * u + 1) * rows]
            odd = r[(2 * u + 1) * rows : (2 * u + 2) * rows]
            out_ref[g * (GROUP // 2) + u] = jnp.where(first_half, even, odd)
        return carry

    lax.fori_loop(0, rows // GROUP, step, 0)


def triples(a, b, w, scale):
    rows, fields = b.shape
    return pl.pallas_call(
        lambda *refs: triple_kernel(scale, *refs),
        name="triples",
        out_shape=jax.ShapeDtypeStruct((rows // 2, rows, 2 * rows), jnp.float32),
        in_specs=in_vmem(3),
        out_specs=pl.BlockSpec(memory_space=pltpu.VMEM),
        compiler_params=pltpu.CompilerParams(vmem_limit_bytes=40 * 2**20),
        cost_estimate=pl.CostEstimate(
            flops=8 * rows**3 * fields, bytes_accessed=4 * (rows**3 + 3 * rows * fields), transcendentals=0
        ),
    )(a, b, w)


def regroup_kernel(arrived_ref, send_ref, own_ref, other_ref, sum_ref):
    pairs, rows, _ = sum_ref.shape
    per_owner = rows // send_ref.shape[0]
    sum_ref[...] = jnp.sum(arrived_ref[...], axis=0)
    for g in range(send_ref.shape[0]):
        for p in range(pairs):
            send_ref[g, p * per_owner : (p + 1) * per_owner] = sum_ref[p, g * per_owner : (g + 1) * per_owner]
    half = lax.rem(lax.axis_index("field"), 2)
    for p in range(pairs // 2):
        own_ref[p] = sum_ref[half * (pairs // 2) + p]
        other_ref[p] = sum_ref[(1 - half) * (pairs // 2) + p]


def regroup(arrived, parts):
    _, pairs, rows, lanes = arrived.shape
    kept = jax.ShapeDtypeStruct((pairs // 2, rows, lanes), jnp.float32)
    return pl.pallas_call(
        regroup_kernel,
        name="regroup",
        out_shape=(jax.ShapeDtypeStruct((parts, pairs * rows // parts, lanes), jnp.float32), kept, kept),
        in_specs=in_vmem(1),
        out_specs=tuple(in_vmem(3)),
        scratch_shapes=[pltpu.VMEM((pairs, rows, lanes), jnp.float32)],
        compiler_params=pltpu.CompilerParams(vmem_limit_bytes=8 * 2**20),
    )(arrived)


def finish_kernel(own_ref, other_ref, turned_ref, first_ref, second_ref, sum_ref, row_ref):
    pairs, rows, lanes = own_ref.shape
    left = lax.broadcasted_iota(jnp.int32, (rows // 2, lanes), 1) < lanes // 2
    for p in range(pairs):
        sum_ref[p * rows : (p + 1) * rows] = own_ref[p] + other_ref[p]
    for p in range(pairs):
        even = sum_ref[pl.ds(p * rows, rows // 2, stride=2), :]
        odd = sum_ref[pl.ds(p * rows + 1, rows // 2, stride=2), :]
        row_ref[p * rows : p * rows + rows // 2] = jnp.where(left, even, pltpu.roll(odd, lanes // 2, 1))
        row_ref[p * rows + rows // 2 : (p + 1) * rows] = jnp.where(left, pltpu.roll(even, lanes // 2, 1), odd)
    for c in range(rows // 2):
        first_ref[:, c * lanes : (c + 1) * lanes] = row_ref[pl.ds(c, 2 * pairs, stride=rows // 2), :]

    parts, height, _ = turned_ref.shape
    per_owner = second_ref.shape[0]
    pairs = height // per_owner
    for z in range(parts // 2):
        for p in range(pairs):
            c = z * pairs + p
            at = slice(p * per_owner, (p + 1) * per_owner)
            second_ref[:, c * lanes : (c + 1) * lanes] = turned_ref[2 * z, at] + turned_ref[2 * z + 1, at]


def finish(own, other, turned):
    pairs, rows, lanes = own.shape
    out = jax.ShapeDtypeStruct((2 * pairs, rows * lanes // 2), jnp.float32)
    return pl.pallas_call(
        finish_kernel,
        name="finish",
        out_shape=(out, out),
        in_specs=in_vmem(3),
        out_specs=tuple(in_vmem(2)),
        scratch_shapes=[pltpu.VMEM((pairs * rows, lanes), jnp.float32)] * 2,
        compiler_params=pltpu.CompilerParams(vmem_limit_bytes=4 * 2**20),
    )(own, other, turned)


def per_device(vectors):
    blocks, parts = lax.axis_size("vec"), lax.axis_size("field")
    rows = vectors.shape[0]
    scale = 1.0 / math.sqrt(vectors.shape[1] * parts)
    line = LINE if blocks % LINE == 0 else blocks
    ends = [((b - 1) % blocks, b) for b in range(0, blocks, line)]
    inner = [(b - 1, b) for b in range(blocks) if b % line]
    turned = lax.ppermute(vectors, "vec", ends + [(b, a) for a, b in ends])
    here = fetched(vectors)
    following = lax.ppermute(vectors, "vec", [(b, a) for a, b in inner])
    previous = lax.ppermute(vectors, "vec", inner)
    spot = lax.rem(lax.axis_index("vec"), line)
    place = [x.astype(jnp.int32).reshape(1) for x in (spot == 0, spot == line - 1)]
    a, w = inputs(place, previous, following, turned)
    partial = triples(a, here, w, scale)
    along_z = [[2 * z + half for z in range(parts // 2)] for half in range(2)]
    pieces = partial.reshape(parts // 2, rows // parts, rows, 2 * rows)
    arrived = lax.all_to_all(pieces, "field", 0, 0, axis_index_groups=along_z, tiled=True)
    send, own, other = regroup(arrived, parts)
    crossed = [(b * parts + f, (b - 1) % blocks * parts + (f ^ 1)) for b in range(blocks) for f in range(parts)]
    turned = lax.all_to_all(send, "field", split_axis=0, concat_axis=0, tiled=True)
    other = lax.ppermute(other, ("vec", "field"), crossed)
    own = passed_along(own, "vec", -1)
    return finish(own, other, turned)


def solution(mesh):
    placed = (P("vec", "field"),)
    return jax.shard_map(
        per_device,
        mesh=mesh,
        in_specs=placed,
        out_specs=(P(("vec", "field"), None), P(("vec", "field"), None)),
        check_vma=False,
    )
```

```python
import functools
import math

import jax
import jax.numpy as jnp
from jax import lax
from jax.experimental import pallas as pl
from jax.experimental.pallas import tpu as pltpu
from jax.sharding import PartitionSpec as P


GROUP = 16


def passed_along(x, axis, by):
    peers = lax.axis_size(axis)
    return lax.ppermute(x, axis, [(i, (i + by) % peers) for i in range(peers)])


def two_halves(x):
    high = x.astype(jnp.bfloat16)
    return high, (x - high.astype(jnp.float32)).astype(jnp.bfloat16)


def in_vmem(count):
    return [pl.BlockSpec(memory_space=pltpu.VMEM)] * count


def fetch_kernel(parity_ref, in_ref, out_ref, early_ref, late_ref, *, run):
    out_ref[...] = in_ref[...]
    for m in range(early_ref.shape[0] // run):
        at = pl.ds(m * run, run)
        early_ref[at, :] = in_ref[pl.ds(pl.multiple_of(2 * m * run + (1 - parity_ref[0]) * run, run), run), :]
        late_ref[at, :] = in_ref[pl.ds(pl.multiple_of(2 * m * run + parity_ref[0] * run, run), run), :]


def fetched(parity, x, run):
    rows, fields = x.shape
    half = jax.ShapeDtypeStruct((rows // 2, fields), x.dtype)
    return pl.pallas_call(
        functools.partial(fetch_kernel, run=run),
        name="fetch",
        out_shape=(jax.ShapeDtypeStruct(x.shape, x.dtype), half, half),
        in_specs=[pl.BlockSpec(memory_space=pltpu.SMEM)] + in_vmem(1),
        out_specs=tuple(in_vmem(3)),
        compiler_params=pltpu.CompilerParams(vmem_limit_bytes=4 * 2**20),
        cost_estimate=pl.CostEstimate(flops=0, bytes_accessed=3 * x.size * 4, transcendentals=0),
    )(parity.reshape(1), x)


def weights_kernel(c_ref, w_ref):
    w_ref[...] = jnp.concatenate(two_halves(c_ref[...]), 0).T


def weights(c):
    rows, fields = c.shape
    return pl.pallas_call(
        weights_kernel,
        name="weights",
        out_shape=jax.ShapeDtypeStruct((fields, 2 * rows), jnp.bfloat16),
        in_specs=in_vmem(1),
        out_specs=pl.BlockSpec(memory_space=pltpu.VMEM),
        compiler_params=pltpu.CompilerParams(vmem_limit_bytes=8 * 2**20),
        cost_estimate=pl.CostEstimate(flops=c.size, bytes_accessed=8 * c.size, transcendentals=0),
    )(c)


def triple_kernel(scale, start, run, stride, a_ref, b_ref, w_ref, out_ref):
    rows = b_ref.shape[0]
    first_half = lax.broadcasted_iota(jnp.int32, (rows, 2 * rows), 1) < rows
    start = start + pl.program_id(0) * (GROUP // run * stride)
    highs, lows = [], []
    for u in range(GROUP):
        high, low = two_halves(a_ref[pl.ds(start + u // run * stride + u % run, 1), :] * b_ref[...])
        highs.append(high)
        lows.append(low)
    w = w_ref[...]
    r = jnp.dot(jnp.concatenate(highs, 0), w, preferred_element_type=jnp.float32)
    r = r + jnp.dot(jnp.concatenate(lows, 0), w, preferred_element_type=jnp.float32)
    r = (r + pltpu.roll(r, rows, 1)) * scale
    for u in range(GROUP // 2):
        even = r[2 * u * rows : (2 * u + 1) * rows]
        odd = r[(2 * u + 1) * rows : (2 * u + 2) * rows]
        out_ref[u] = jnp.where(first_half, even, odd)


def triples(a, b, w, scale, steps, start, run, stride):
    rows, fields = b.shape
    return pl.pallas_call(
        lambda *refs: triple_kernel(scale, start, run, stride, *refs),
        name="triples",
        grid=(steps,),
        out_shape=jax.ShapeDtypeStruct((steps * GROUP // 2, rows, 2 * rows), jnp.float32),
        in_specs=in_vmem(3),
        out_specs=pl.BlockSpec((GROUP // 2, rows, 2 * rows), lambda s: (s, 0, 0)),
        compiler_params=pltpu.CompilerParams(vmem_limit_bytes=40 * 2**20),
        cost_estimate=pl.CostEstimate(
            flops=8 * steps * GROUP * rows**2 * fields,
            bytes_accessed=4 * (steps * GROUP * rows**2 + 3 * rows * fields),
            transcendentals=0,
        ),
    )(a, b, w)


def merge_kernel(mine_ref, theirs_ref, *refs):
    refs[-1][...] = mine_ref[...] + theirs_ref[...]


def merge(mine, theirs, part, held=None):
    owners, _, pairs, rows, lanes = mine.shape
    block = pl.BlockSpec((owners, 1, pairs, rows, lanes), lambda step: (0, part, 0, 0, 0))
    whole = pl.BlockSpec((owners, 1, pairs, rows, lanes), lambda step: (0, 0, 0, 0, 0))
    more = () if held is None else (held,)
    return pl.pallas_call(
        merge_kernel,
        name="merge",
        grid=(1,),
        out_shape=jax.ShapeDtypeStruct(mine.shape, jnp.float32),
        in_specs=[block, whole] + [pl.BlockSpec(memory_space=pl.ANY)] * len(more),
        out_specs=block,
        input_output_aliases={2: 0} if more else {},
        compiler_params=pltpu.CompilerParams(vmem_limit_bytes=8 * 2**20),
    )(mine, theirs.reshape(owners, 1, pairs, rows, lanes), *more)


def regroup_kernel(arrived_ref, send_ref, own_ref, other_ref, sum_ref):
    pairs, rows, _ = sum_ref.shape
    per_owner = rows // send_ref.shape[0]
    sum_ref[...] = jnp.sum(arrived_ref[...], axis=0)
    for g in range(send_ref.shape[0]):
        for p in range(pairs):
            send_ref[g, p * per_owner : (p + 1) * per_owner] = sum_ref[p, g * per_owner : (g + 1) * per_owner]
    half = lax.rem(lax.axis_index("field"), 2)
    for p in range(pairs // 2):
        own_ref[p] = sum_ref[half * (pairs // 2) + p]
        other_ref[p] = sum_ref[(1 - half) * (pairs // 2) + p]


def regroup(arrived, parts):
    _, pairs, rows, lanes = arrived.shape
    kept = jax.ShapeDtypeStruct((pairs // 2, rows, lanes), jnp.float32)
    return pl.pallas_call(
        regroup_kernel,
        name="regroup",
        out_shape=(jax.ShapeDtypeStruct((parts, pairs * rows // parts, lanes), jnp.float32), kept, kept),
        in_specs=in_vmem(1),
        out_specs=tuple(in_vmem(3)),
        scratch_shapes=[pltpu.VMEM((pairs, rows, lanes), jnp.float32)],
        compiler_params=pltpu.CompilerParams(vmem_limit_bytes=8 * 2**20),
    )(arrived)


def finish_kernel(own_ref, other_ref, turned_ref, first_ref, second_ref, sum_ref, row_ref):
    pairs, rows, lanes = own_ref.shape
    left = lax.broadcasted_iota(jnp.int32, (rows // 2, lanes), 1) < lanes // 2
    for p in range(pairs):
        sum_ref[p * rows : (p + 1) * rows] = own_ref[p] + other_ref[p]
    for p in range(pairs):
        even = sum_ref[pl.ds(p * rows, rows // 2, stride=2), :]
        odd = sum_ref[pl.ds(p * rows + 1, rows // 2, stride=2), :]
        row_ref[p * rows : p * rows + rows // 2] = jnp.where(left, even, pltpu.roll(odd, lanes // 2, 1))
        row_ref[p * rows + rows // 2 : (p + 1) * rows] = jnp.where(left, pltpu.roll(even, lanes // 2, 1), odd)
    for c in range(rows // 2):
        first_ref[:, c * lanes : (c + 1) * lanes] = row_ref[pl.ds(c, 2 * pairs, stride=rows // 2), :]

    parts, height, _ = turned_ref.shape
    per_owner = second_ref.shape[0]
    pairs = height // per_owner
    for z in range(parts // 2):
        for p in range(pairs):
            c = z * pairs + p
            at = slice(p * per_owner, (p + 1) * per_owner)
            second_ref[:, c * lanes : (c + 1) * lanes] = turned_ref[2 * z, at] + turned_ref[2 * z + 1, at]


def finish(own, other, turned):
    pairs, rows, lanes = own.shape
    out = jax.ShapeDtypeStruct((2 * pairs, rows * lanes // 2), jnp.float32)
    return pl.pallas_call(
        finish_kernel,
        name="finish",
        out_shape=(out, out),
        in_specs=in_vmem(3),
        out_specs=tuple(in_vmem(2)),
        scratch_shapes=[pltpu.VMEM((pairs * rows, lanes), jnp.float32)] * 2,
        compiler_params=pltpu.CompilerParams(vmem_limit_bytes=4 * 2**20),
    )(own, other, turned)


def per_device(vectors):
    blocks, parts = lax.axis_size("vec"), lax.axis_size("field")
    rows = vectors.shape[0]
    scale = 1.0 / math.sqrt(vectors.shape[1] * parts)
    peers = parts // 2
    run = rows // peers
    following = passed_along(vectors, "vec", -1)
    here, early, late = fetched(lax.axis_index("field") // 2 % 2, vectors, run)
    early = passed_along(early, "vec", 1)
    late = passed_along(late, "vec", 1)
    w = weights(following)

    def sent(part, towards):
        sums = triples(early, here, w, scale, rows // 4 // GROUP, part * (run // 2), run // 2, run)
        moves = [(2 * z + half, 2 * (towards(z) % peers) + half) for z in range(peers) for half in range(2)]
        return lax.ppermute(sums, "field", moves)

    low = sent(0, lambda z: z ^ 1)
    high = sent(1, lambda z: z + 1 if z % 2 else z - 1)
    mine = triples(late, here, w, scale, rows // 2 // GROUP, 0, run, run)
    mine = mine.reshape(peers // 2, 2, run // 4, rows, 2 * rows)
    merged = merge(mine, high, 1, merge(mine, low, 0))
    along_z = [[2 * z + half for z in range(q, peers, 2)] for q in range(2) for half in range(2)]
    pieces = merged.reshape(peers // 2, run // 2, rows, 2 * rows)
    arrived = lax.all_to_all(pieces, "field", 0, 0, axis_index_groups=along_z, tiled=True)
    send, own, other = regroup(arrived, parts)
    crossed = [(b * parts + f, (b - 1) % blocks * parts + (f ^ 1)) for b in range(blocks) for f in range(parts)]
    turned = lax.all_to_all(send, "field", split_axis=0, concat_axis=0, tiled=True)
    other = lax.ppermute(other, ("vec", "field"), crossed)
    own = passed_along(own, "vec", -1)
    return finish(own, other, turned)


def solution(mesh):
    placed = (P("vec", "field"),)
    return jax.shard_map(
        per_device,
        mesh=mesh,
        in_specs=placed,
        out_specs=(P(("vec", "field"), None), P(("vec", "field"), None)),
        check_vma=False,
    )
```
